32 devices in a mesh: fsdp: 8 (over y, x, core), tp: 4 (over z).
Axes of the slice: x: 2, y: 2, z: 4, core: 2. Of those that a mesh axis runs over, the one named last changes fastest.
Arguments:
- layer_input: bfloat16 [8192, 2048], P(('fsdp', 'tp')), may hold values from -6 to 6
- segments: int32 [16, 512], P('fsdp'), may hold values from 0 to 7, never falling along the last dimension, each value on 1 to 256 neighbouring positions
- cotangent: bfloat16 [8192, 2048], P(('fsdp', 'tp')), may hold values from -6 to 6
- attention_gain: float32 [2048], replicated, may hold values from 0.1 to 1.9
- query_weight: bfloat16 [2048, 2048], P('fsdp', 'tp'), may hold values from -0.125 to 0.125
- key_matrix: bfloat16 [2048, 1024], P('fsdp', 'tp'), may hold values from -0.125 to 0.125
- value_matrix: bfloat16 [2048, 1024], P('fsdp', 'tp'), may hold values from -0.125 to 0.125
- query_norm_gain: float32 [128], replicated, may hold values from 0.1 to 1.9
- key_gain: float32 [128], replicated, may hold values from 0.1 to 1.9
- output_matrix: bfloat16 [2048, 2048], P('tp', 'fsdp'), may hold values from -1 to 1
- hidden_gain: float32 [2048], replicated, may hold values from 0.1 to 1.9
- gate_weight: bfloat16 [2048, 6144], P('fsdp', 'tp'), may hold values from -0.125 to 0.125
- up_weight: bfloat16 [2048, 6144], P('fsdp', 'tp'), may hold values from -0.125 to 0.125
- down_weight: bfloat16 [6144, 2048], P('tp', 'fsdp'), may hold values from -0.078125 to 0.078125
Outputs:
- layer_output: bfloat16 [8192, 2048], P(('fsdp', 'tp'))
- input_gradient: bfloat16 [8192, 2048], P(('fsdp', 'tp'))
- attention_gain_gradient: float32 [2048], replicated
- query_weight_gradient: float32 [2048, 2048], P('fsdp', 'tp')
- key_weight_gradient: float32 [2048, 1024], P('fsdp', 'tp')
- value_weight_gradient: float32 [2048, 1024], P('fsdp', 'tp')
- query_gain_gradient: float32 [128], replicated
- key_gain_gradient: float32 [128], replicated
- output_weight_gradient: float32 [2048, 2048], P('tp', 'fsdp')
- hidden_gain_gradient: float32 [2048], replicated
- gate_weight_gradient: float32 [2048, 6144], P('fsdp', 'tp')
- up_weight_gradient: float32 [2048, 6144], P('fsdp', 'tp')
- down_weight_gradient: float32 [6144, 2048], P('tp', 'fsdp')
The draws below stay inside these ranges and needn't reach their ends.
Inputs may be any that keep to these rules, and one draw needn't show every extreme that they name: `segments`: within each sequence the ids never fall along positions and all 8 ids occur; each document holds 1 to 256 tokens, and some document holds exactly 256.
All inputs are finite; a program needn't handle non-finite values.
Results may differ from the reference program's by a relative error of at most 0.014.
Values may be sent and summed in bfloat16 or wider, within the bound.
No kernel may reach another device: no remote copies, remote signals or barrier semaphores. Data moves between devices by JAX's collectives and lax.ppermute only.
A program may use at most 256 MiB of HBM per device.

```python
import math
from functools import partial
import jax
import jax.numpy as jnp
import numpy as np
from jax import lax

MODEL_WIDTH = 2048
QUERY_HEADS = 16
KEY_VALUE_HEADS = 8
HEAD_SIZE = 128
HIDDEN_UNITS = 6144
PACKED_TOKENS = 512
TOKENS = 8192
NSEQ = 16


def steps_of(stream_key, extent, split, low, top_value):
    gain, own = 1.0, jax.random.fold_in(stream_key, 6)
    for position, blocks in split:
        draws = jnp.exp(jax.random.uniform(jax.random.fold_in(own, position), (blocks,), jnp.float32, low / len(split), top_value / len(split)))
        gain = gain * jnp.repeat(draws, extent[position] // blocks).reshape([-1 if axis == position else 1 for axis in range(len(extent))])
    return gain


def split_up(number_of, total, limit, skew):
    loads = [(1 << 20) // math.isqrt(rank ** skew) + 1 for rank in range(2, number_of + 1)]
    spare, given = total - limit - (number_of - 1), [1] * (number_of - 1)
    while spare > 0:
        candidates = [i for i in range(number_of - 1) if given[i] < limit]
        mass, remaining = sum([loads[i] for i in candidates]), spare
        for i in candidates:
            addition = min(limit - given[i], max(1, remaining * loads[i] // mass), spare)
            given[i] = given[i] + addition
            spare = spare - addition
    return np.array([limit] + given)


def ragged_sizes(rng, number_of, total, most, lean):
    if number_of == 2:
        one = jax.random.randint(rng, (), max(1, total - most), min(most, total - 1) + 1)
        return jnp.stack([one, total - one])
    tallies = jnp.asarray(split_up(number_of, total, most, lean), jnp.int32)
    pairs = (number_of - 1) // 2
    source_of, taker = tallies[1:1 + 2 * pairs:2], tallies[2:2 + 2 * pairs:2]
    room = jnp.minimum(source_of - 1, most - taker)
    passed = jax.random.randint(jax.random.fold_in(rng, 1), (pairs,), 0, 1 << 20) % (room + 1)
    tallies = tallies.at[1:1 + 2 * pairs:2].set(source_of - passed).at[2:2 + 2 * pairs:2].set(taker + passed)
    return tallies[jax.random.permutation(jax.random.fold_in(rng, 2), number_of)]


def centred(key, extent, scale, limit, split=(), kind=jnp.bfloat16):
    array = scale * jax.random.normal(key, extent, jnp.float32)
    if split:
        array = array * steps_of(key, extent, split, -0.22, 0.18)
    return jnp.clip(array, -limit, limit).astype(kind)


def setup_inputs(seed: int = 0) -> dict:
    streams_of = jax.random.split(jax.random.key(seed), 15)
    return {
        "layer_input": centred(streams_of[0], (TOKENS, MODEL_WIDTH), 1.0, 6.0, ((0, 32),)),
        "segments": jax.vmap(lambda own: jnp.searchsorted(jnp.cumsum(ragged_sizes(own, 8, PACKED_TOKENS, PACKED_TOKENS // 2, 0)), jnp.arange(PACKED_TOKENS), side="right"))(jax.random.split(streams_of[1], NSEQ)).reshape((NSEQ, PACKED_TOKENS)).astype(jnp.int32),
        "cotangent": centred(streams_of[2], (TOKENS, MODEL_WIDTH), 1.0, 6.0, ((0, 32),)),
        "attention_gain": jnp.clip(1.0 + 0.18 * jax.random.normal(streams_of[3], (MODEL_WIDTH,), jnp.float32), 0.1, 1.9),
        "query_weight": centred(streams_of[4], (MODEL_WIDTH, QUERY_HEADS * HEAD_SIZE), MODEL_WIDTH ** -0.5, 0.125, ((0, 8), (1, 4))),
        "key_matrix": centred(streams_of[5], (MODEL_WIDTH, KEY_VALUE_HEADS * HEAD_SIZE), MODEL_WIDTH ** -0.5, 0.125, ((0, 8), (1, 4))),
        "value_matrix": centred(streams_of[6], (MODEL_WIDTH, KEY_VALUE_HEADS * HEAD_SIZE), MODEL_WIDTH ** -0.5, 0.125, ((0, 8), (1, 4))),
        "query_norm_gain": jnp.clip(1.0 + 0.18 * jax.random.normal(streams_of[7], (HEAD_SIZE,), jnp.float32), 0.1, 1.9),
        "key_gain": jnp.clip(1.0 + 0.18 * jax.random.normal(streams_of[8], (HEAD_SIZE,), jnp.float32), 0.1, 1.9),
        "output_matrix": centred(streams_of[9], (QUERY_HEADS * HEAD_SIZE, MODEL_WIDTH), (QUERY_HEADS * HEAD_SIZE // 64) ** -0.5, 1.0, ((0, 4), (1, 8))),
        "hidden_gain": jnp.clip(1.0 + 0.18 * jax.random.normal(streams_of[10], (MODEL_WIDTH,), jnp.float32), 0.1, 1.9),
        "gate_weight": centred(streams_of[11], (MODEL_WIDTH, HIDDEN_UNITS), MODEL_WIDTH ** -0.5, 0.125, ((0, 8), (1, 4))),
        "up_weight": centred(streams_of[12], (MODEL_WIDTH, HIDDEN_UNITS), MODEL_WIDTH ** -0.5, 0.125, ((0, 8), (1, 4))),
        "down_weight": centred(streams_of[13], (HIDDEN_UNITS, MODEL_WIDTH), HIDDEN_UNITS ** -0.5, 0.078125, ((0, 4), (1, 8))),
    }


EPSILON = 1e-06
THETA = 1000000.0

def rms_scale(value_rows, norm_gain):
    return value_rows * lax.rsqrt(lax.optimization_barrier(jnp.mean(value_rows * value_rows, axis=-1, keepdims=True)) + EPSILON) * norm_gain

def doc_positions(segments):
    length = segments.shape[-1]
    indices = jnp.arange(length, dtype=jnp.int32)
    leading = jnp.ones(segments.shape[:-1] + (1,), dtype=jnp.bool_)
    change = jnp.concatenate([leading, segments[..., 1:] != segments[..., :-1]], axis=-1)
    starts = lax.cummax(jnp.where(change, indices, jnp.int32(0)), axis=segments.ndim - 1)
    return (indices - starts).astype(jnp.int32)

def rotate(vectors, token_positions):
    half_dim = vectors.shape[-1] // 2
    exponents = jnp.arange(half_dim, dtype=jnp.float32) * (-2.0 / vectors.shape[-1])
    frequencies = jnp.power(jnp.float32(THETA), exponents)
    angles = token_positions.astype(jnp.float32)[..., None] * frequencies
    cosine_table = jnp.cos(angles)[..., None, :]
    sine_table = jnp.sin(angles)[..., None, :]
    first_half = vectors[..., :half_dim]
    second_half = vectors[..., half_dim:]
    return jnp.concatenate([first_half * cosine_table - second_half * sine_table, second_half * cosine_table + first_half * sine_table], axis=-1)

def head_lookup(raw_heads, norm_gain, token_positions):
    return rotate(rms_scale(raw_heads, norm_gain), token_positions)

def contract_product(left_side, right_side, left_dim, right_dim):
    return lax.dot_general(left_side, right_side, (((left_dim,), (right_dim,)), ((), ())), preferred_element_type=jnp.float32)

def attend_mask(segments):
    length = segments.shape[0]
    indices = jnp.arange(length, dtype=jnp.int32)
    causal = indices[:, None] >= indices[None, :]
    return causal & (segments[:, None] == segments[None, :])

def attend_forward(query_rows, keys, value_rows, segments):
    score_scale = 1.0 / math.sqrt(query_rows.shape[-1])
    scores = jnp.einsum('qkgd,ckd->kgqc', query_rows.astype(jnp.float32), keys.astype(jnp.float32)) * score_scale
    allowed = attend_mask(segments)
    exponent = jnp.where(allowed, jnp.exp(scores), 0.0)
    log_total = jnp.log(lax.optimization_barrier(jnp.sum(exponent, axis=-1)))
    probability = jnp.where(allowed, jnp.exp(scores - log_total[..., None]), 0.0).astype(jnp.bfloat16)
    attended = jnp.einsum('kgqc,ckd->qkgd', probability.astype(jnp.float32), value_rows.astype(jnp.float32)).astype(jnp.bfloat16)
    return (attended, log_total)

def attend_backward(query_rows, keys, value_rows, segments, log_total, attended, attended_gradient):
    score_scale = 1.0 / math.sqrt(query_rows.shape[-1])
    query_float = query_rows.astype(jnp.float32)
    key_float = keys.astype(jnp.float32)
    back_float = attended_gradient.astype(jnp.float32)
    scores = jnp.einsum('qkgd,ckd->kgqc', query_float, key_float) * score_scale
    allowed = attend_mask(segments)
    probability = jnp.where(allowed, jnp.exp(scores - log_total[..., None]), 0.0)
    prob_low = probability.astype(jnp.bfloat16)
    delta = jnp.einsum('qkgd,qkgd->kgq', back_float, attended.astype(jnp.float32))
    value_dots = jnp.einsum('qkgd,ckd->kgqc', back_float, value_rows.astype(jnp.float32))
    score_back = (probability * (value_dots - delta[..., None])).astype(jnp.bfloat16)
    score_float = score_back.astype(jnp.float32)
    query_back = jnp.einsum('kgqc,ckd->qkgd', score_float, key_float) * score_scale
    key_back = jnp.einsum('kgqc,qkgd->ckd', score_float, query_float) * score_scale
    value_gradient = jnp.einsum('kgqc,qkgd->ckd', prob_low.astype(jnp.float32), back_float).astype(jnp.bfloat16)
    return (query_back, key_back, value_gradient)

def reference(layer_input, segments, cotangent, attention_gain, query_weight, key_matrix, value_matrix, query_norm_gain, key_gain, output_matrix, hidden_gain, gate_weight, up_weight, down_weight):
    each_block = math.gcd(NSEQ, 8)
    block_count = NSEQ // each_block
    rows_per_block = each_block * PACKED_TOKENS
    each_group = QUERY_HEADS // KEY_VALUE_HEADS
    inputs_blocked = layer_input.reshape(block_count, rows_per_block, MODEL_WIDTH)
    segments_blocked = segments.reshape(block_count, each_block, PACKED_TOKENS)
    cotangent_blocked = cotangent.reshape(block_count, rows_per_block, MODEL_WIDTH)

    def one_block(carry, items):
        block_input, block_segments, block_cotangent = items
        token_positions = doc_positions(block_segments)
        input_float = block_input.astype(jnp.float32)
        attention_input = rms_scale(input_float, attention_gain).astype(jnp.bfloat16)
        query_unnormed = jnp.dot(attention_input, query_weight, preferred_element_type=jnp.float32).reshape(each_block, PACKED_TOKENS, QUERY_HEADS, HEAD_SIZE)
        key_unnormed = jnp.dot(attention_input, key_matrix, preferred_element_type=jnp.float32).reshape(each_block, PACKED_TOKENS, KEY_VALUE_HEADS, HEAD_SIZE)
        value_rows = jnp.dot(attention_input, value_matrix, preferred_element_type=jnp.float32).astype(jnp.bfloat16).reshape(each_block, PACKED_TOKENS, KEY_VALUE_HEADS, HEAD_SIZE)
        query_rows = head_lookup(query_unnormed, query_norm_gain, token_positions).astype(jnp.bfloat16).reshape(each_block, PACKED_TOKENS, KEY_VALUE_HEADS, each_group, HEAD_SIZE)
        keys = head_lookup(key_unnormed, key_gain, token_positions).astype(jnp.bfloat16)
        attended, log_total = jax.vmap(attend_forward)(query_rows, keys, value_rows, block_segments)
        attended_flat = attended.reshape(rows_per_block, QUERY_HEADS * HEAD_SIZE)
        mid = input_float + jnp.dot(attended_flat, output_matrix, preferred_element_type=jnp.float32)
        hidden_in = rms_scale(mid, hidden_gain).astype(jnp.bfloat16)
        gate_value = jnp.dot(hidden_in, gate_weight, preferred_element_type=jnp.float32)
        up_value = jnp.dot(hidden_in, up_weight, preferred_element_type=jnp.float32)
        hidden = (jax.nn.silu(gate_value) * up_value).astype(jnp.bfloat16)
        block_output = (mid + jnp.dot(hidden, down_weight, preferred_element_type=jnp.float32)).astype(jnp.bfloat16)
        hidden_back = contract_product(block_cotangent, down_weight, 1, 1)
        sigmoid = jax.nn.sigmoid(gate_value)
        gate_back = (hidden_back * up_value * sigmoid * (1.0 + gate_value * (1.0 - sigmoid))).astype(jnp.bfloat16)
        upward_back = (hidden_back * gate_value * sigmoid).astype(jnp.bfloat16)
        down_part = contract_product(hidden, block_cotangent, 0, 0)
        gate_part = contract_product(hidden_in, gate_back, 0, 0)
        up_part = contract_product(hidden_in, upward_back, 0, 0)
        hidden_in_back = contract_product(gate_back, gate_weight, 1, 1) + contract_product(upward_back, up_weight, 1, 1)
        mid_part, hidden_gain_part = jax.vjp(rms_scale, mid, hidden_gain)[1](hidden_in_back)
        mid_back = block_cotangent.astype(jnp.float32) + mid_part
        mixer_gradient = mid_back.astype(jnp.bfloat16)
        output_part = contract_product(attended_flat, mixer_gradient, 0, 0)
        attended_gradient = contract_product(mixer_gradient, output_matrix, 1, 1).astype(jnp.bfloat16).reshape(each_block, PACKED_TOKENS, KEY_VALUE_HEADS, each_group, HEAD_SIZE)
        query_back, key_back, value_gradient = jax.vmap(attend_backward)(query_rows, keys, value_rows, block_segments, log_total, attended, attended_gradient)
        query_back = query_back.reshape(each_block, PACKED_TOKENS, QUERY_HEADS, HEAD_SIZE)
        query_raw_back, query_gain_part = jax.vjp(partial(head_lookup, token_positions=token_positions), query_unnormed, query_norm_gain)[1](query_back)
        key_unnormed_gradient, key_gain_part = jax.vjp(partial(head_lookup, token_positions=token_positions), key_unnormed, key_gain)[1](key_back)
        query_low = query_raw_back.astype(jnp.bfloat16).reshape(rows_per_block, QUERY_HEADS * HEAD_SIZE)
        key_reduced = key_unnormed_gradient.astype(jnp.bfloat16).reshape(rows_per_block, KEY_VALUE_HEADS * HEAD_SIZE)
        value_reduced = value_gradient.reshape(rows_per_block, KEY_VALUE_HEADS * HEAD_SIZE)
        query_part = contract_product(attention_input, query_low, 0, 0)
        key_part = contract_product(attention_input, key_reduced, 0, 0)
        value_part = contract_product(attention_input, value_reduced, 0, 0)
        attention_in_back = contract_product(query_low, query_weight, 1, 1) + contract_product(key_reduced, key_matrix, 1, 1) + contract_product(value_reduced, value_matrix, 1, 1)
        input_part, attention_gain_part = jax.vjp(rms_scale, input_float, attention_gain)[1](attention_in_back)
        block_gradient = (mid_back + input_part).astype(jnp.bfloat16)
        parts = (attention_gain_part, query_part, key_part, value_part, query_gain_part, key_gain_part, output_part, hidden_gain_part, gate_part, up_part, down_part)
        return (jax.tree.map(jnp.add, carry, parts), (block_output, block_gradient))
    document_start_sums = (jnp.zeros((MODEL_WIDTH,), jnp.float32), jnp.zeros((MODEL_WIDTH, QUERY_HEADS * HEAD_SIZE), jnp.float32), jnp.zeros((MODEL_WIDTH, KEY_VALUE_HEADS * HEAD_SIZE), jnp.float32), jnp.zeros((MODEL_WIDTH, KEY_VALUE_HEADS * HEAD_SIZE), jnp.float32), jnp.zeros((HEAD_SIZE,), jnp.float32), jnp.zeros((HEAD_SIZE,), jnp.float32), jnp.zeros((QUERY_HEADS * HEAD_SIZE, MODEL_WIDTH), jnp.float32), jnp.zeros((MODEL_WIDTH,), jnp.float32), jnp.zeros((MODEL_WIDTH, HIDDEN_UNITS), jnp.float32), jnp.zeros((MODEL_WIDTH, HIDDEN_UNITS), jnp.float32), jnp.zeros((HIDDEN_UNITS, MODEL_WIDTH), jnp.float32))
    sums, (outputs, gradients) = lax.scan(one_block, document_start_sums, (inputs_blocked, segments_blocked, cotangent_blocked))
    return (outputs.reshape(TOKENS, MODEL_WIDTH), gradients.reshape(TOKENS, MODEL_WIDTH), sums[0], sums[1], sums[2], sums[3], sums[4], sums[5], sums[6], sums[7], sums[8], sums[9], sums[10])
```

```python
import math
from functools import partial

import jax
import jax.numpy as jnp
from jax import lax
from jax.sharding import PartitionSpec as P

EPSILON = 1e-06
THETA = 1000000.0


def rms_scale(value_rows, norm_gain):
    return (
        value_rows
        * lax.rsqrt(jnp.mean(value_rows * value_rows, axis=-1, keepdims=True) + EPSILON)
        * norm_gain
    )


def doc_positions(segments):
    length = segments.shape[-1]
    indices = jnp.arange(length, dtype=jnp.int32)
    leading = jnp.ones(segments.shape[:-1] + (1,), dtype=jnp.bool_)
    change = jnp.concatenate([leading, segments[..., 1:] != segments[..., :-1]], axis=-1)
    starts = lax.cummax(jnp.where(change, indices, jnp.int32(0)), axis=segments.ndim - 1)
    return indices - starts


def rotate(vectors, cosine_table, sine_table):
    half_dim = vectors.shape[-1] // 2
    first_half = vectors[..., :half_dim]
    second_half = vectors[..., half_dim:]
    return jnp.concatenate(
        [
            first_half * cosine_table - second_half * sine_table,
            second_half * cosine_table + first_half * sine_table,
        ],
        axis=-1,
    )


def head_lookup(raw_heads, norm_gain, cosine_table, sine_table):
    return rotate(rms_scale(raw_heads, norm_gain), cosine_table, sine_table)


def contract(left_side, right_side, left_dim, right_dim):
    return lax.dot_general(
        left_side,
        right_side,
        (((left_dim,), (right_dim,)), ((), ())),
        preferred_element_type=jnp.float32,
    )


def attend_forward(query_rows, keys, value_rows, allowed):
    score_scale = 1.0 / math.sqrt(query_rows.shape[-1])
    scores = (
        jnp.einsum("qkgd,ckd->kgqc", query_rows, keys, preferred_element_type=jnp.float32)
        * score_scale
    )
    exponent = jnp.where(allowed, jnp.exp(scores), 0.0)
    log_total = jnp.log(jnp.sum(exponent, axis=-1))
    probability = jnp.where(allowed, jnp.exp(scores - log_total[..., None]), 0.0).astype(
        jnp.bfloat16
    )
    attended = jnp.einsum(
        "kgqc,ckd->qkgd", probability, value_rows, preferred_element_type=jnp.float32
    ).astype(jnp.bfloat16)
    return (attended, log_total)


def attend_backward(query_rows, keys, value_rows, allowed, log_total, attended, attended_gradient):
    score_scale = 1.0 / math.sqrt(query_rows.shape[-1])
    scores = (
        jnp.einsum("qkgd,ckd->kgqc", query_rows, keys, preferred_element_type=jnp.float32)
        * score_scale
    )
    probability = jnp.where(allowed, jnp.exp(scores - log_total[..., None]), 0.0)
    prob_low = probability.astype(jnp.bfloat16)
    delta = jnp.einsum(
        "qkgd,qkgd->kgq", attended_gradient, attended, preferred_element_type=jnp.float32
    )
    value_dots = jnp.einsum(
        "qkgd,ckd->kgqc", attended_gradient, value_rows, preferred_element_type=jnp.float32
    )
    score_back = (probability * (value_dots - delta[..., None])).astype(jnp.bfloat16)
    query_back = (
        jnp.einsum("kgqc,ckd->qkgd", score_back, keys, preferred_element_type=jnp.float32)
        * score_scale
    )
    key_back = (
        jnp.einsum("kgqc,qkgd->ckd", score_back, query_rows, preferred_element_type=jnp.float32)
        * score_scale
    )
    value_gradient = jnp.einsum(
        "kgqc,qkgd->ckd", prob_low, attended_gradient, preferred_element_type=jnp.float32
    ).astype(jnp.bfloat16)
    return (query_back, key_back, value_gradient)


def shards(
    sizes,
    layer_input,
    segments,
    cotangent,
    attention_gain,
    query_weight,
    key_matrix,
    value_matrix,
    query_norm_gain,
    key_gain,
    output_matrix,
    hidden_gain,
    gate_weight,
    up_weight,
    down_weight,
):
    fsdp, tp = sizes
    low = jnp.bfloat16
    own_rows, width = layer_input.shape
    seq_count, seq_length = segments.shape
    head_size = query_norm_gain.shape[0]
    team = tp // seq_count
    sets = seq_count
    me = lax.axis_index("tp")
    place = me % team

    def hop(value, step):
        return lax.ppermute(value, "tp", [(i, (i + step) % tp) for i in range(tp)])

    def team_hop(value, step):
        return lax.ppermute(
            value, "tp", [(i, i // team * team + (i + step) % team) for i in range(tp)]
        )

    def team_rows(own):
        return jnp.concatenate([own] + [team_hop(own, step) for step in range(1, team)], axis=0)

    def team_sum(partial_rows):
        total = partial_rows[:own_rows]
        for step in range(1, team):
            block = partial_rows[step * own_rows : (step + 1) * own_rows].astype(low)
            total = total + team_hop(block, team - step).astype(jnp.float32)
        return total

    def ring_rows(own):
        blocks = [own]
        for _ in range(1, tp):
            blocks.append(hop(blocks[-1], 1))
        return blocks

    def ring_sum(blocks):
        carried = blocks[1]
        for step in range(2, tp + 1):
            carried = hop(carried.astype(low), 1).astype(jnp.float32) + blocks[step % tp]
        return carried

    input_float = layer_input.astype(jnp.float32)
    attention_input = rms_scale(input_float, attention_gain).astype(low)
    attention_rows = team_rows(attention_input)

    own_set = jnp.concatenate(
        [query_weight, key_matrix, value_matrix, output_matrix.T], axis=1
    )
    weight_sets = [own_set] + [
        lax.ppermute(
            own_set,
            "tp",
            [(i, (i // team + m) % sets * team + i % team) for i in range(tp)],
        )
        for m in range(1, sets)
    ]
    set_full = [lax.all_gather(w, "fsdp", axis=0, tiled=True) for w in weight_sets]
    gate_full = lax.all_gather(gate_weight, "fsdp", axis=0, tiled=True)
    up_full = lax.all_gather(up_weight, "fsdp", axis=0, tiled=True)
    down_full = lax.all_gather(down_weight, "fsdp", axis=1, tiled=True)

    query_width = query_weight.shape[1]
    key_width = key_matrix.shape[1]
    mix_width = query_width + 2 * key_width
    local_queries = query_width // head_size
    local_keys = key_width // head_size
    each_group = local_queries // local_keys

    own_segments = lax.dynamic_index_in_dim(segments, me // team, 0, keepdims=False)
    own_positions = doc_positions(own_segments)
    blocks = [
        (place + team - step) % team * own_rows + jnp.arange(own_rows, dtype=jnp.int32)
        for step in range(team)
    ]
    tokens = jnp.concatenate(blocks)
    row_segments = own_segments[tokens]
    row_positions = own_positions[tokens]
    allowed = (tokens[:, None] >= tokens[None, :]) & (
        row_segments[:, None] == row_segments[None, :]
    )
    exponents = jnp.arange(head_size // 2, dtype=jnp.float32) * (-2.0 / head_size)
    frequencies = jnp.power(jnp.float32(THETA), exponents)
    angles = row_positions.astype(jnp.float32)[:, None] * frequencies
    cosine_table = jnp.cos(angles)[:, None, :]
    sine_table = jnp.sin(angles)[:, None, :]

    saved = []
    mixed = None
    for full in set_full:
        raw = jnp.dot(attention_rows, full[:, :mix_width], preferred_element_type=jnp.float32)
        query_raw = raw[:, :query_width].reshape(seq_length, local_queries, head_size)
        key_raw = raw[:, query_width : query_width + key_width].reshape(
            seq_length, local_keys, head_size
        )
        value_rows = (
            raw[:, query_width + key_width :].astype(low).reshape(seq_length, local_keys, head_size)
        )
        query_rows = (
            head_lookup(query_raw, query_norm_gain, cosine_table, sine_table)
            .astype(low)
            .reshape(seq_length, local_keys, each_group, head_size)
        )
        keys = head_lookup(key_raw, key_gain, cosine_table, sine_table).astype(low)
        attended, log_total = attend_forward(query_rows, keys, value_rows, allowed)
        saved.append((query_raw, key_raw, query_rows, keys, value_rows, attended, log_total))
        attended_flat = attended.reshape(seq_length, query_width)
        term = contract(attended_flat, full[:, mix_width:], 1, 1)
        mixed = term if mixed is None else mixed + term

    mid = input_float + team_sum(mixed)
    hidden_in = rms_scale(mid, hidden_gain).astype(low)

    cotangent_blocks = ring_rows(cotangent)
    hidden_blocks = ring_rows(hidden_in)
    out_parts, in_parts, hiddens, gate_backs, up_backs = [], [], [], [], []
    for cotangent_rows, hidden_rows in zip(cotangent_blocks, hidden_blocks):
        gate_value = jnp.dot(hidden_rows, gate_full, preferred_element_type=jnp.float32)
        up_value = jnp.dot(hidden_rows, up_full, preferred_element_type=jnp.float32)
        hidden_back = contract(cotangent_rows, down_full, 1, 1)
        sigmoid = jax.nn.sigmoid(gate_value)
        hidden = (gate_value * sigmoid * up_value).astype(low)
        gate_back = (
            hidden_back * up_value * sigmoid * (1.0 + gate_value * (1.0 - sigmoid))
        ).astype(low)
        up_back = (hidden_back * gate_value * sigmoid).astype(low)
        hiddens.append(hidden)
        gate_backs.append(gate_back)
        up_backs.append(up_back)
        in_parts.append(contract(gate_back, gate_full, 1, 1) + contract(up_back, up_full, 1, 1))
        out_parts.append(jnp.dot(hidden, down_full, preferred_element_type=jnp.float32))

    hidden_in_back = ring_sum(in_parts)
    layer_output = (mid + ring_sum(out_parts)).astype(low)

    hidden_all = jnp.concatenate(hiddens, axis=0)
    gate_back_all = jnp.concatenate(gate_backs, axis=0)
    up_back_all = jnp.concatenate(up_backs, axis=0)
    hidden_in_all = jnp.concatenate(hidden_blocks, axis=0)
    cotangent_all = jnp.concatenate(cotangent_blocks, axis=0)

    def scatter(value, dim):
        return lax.psum_scatter(value.astype(low), "fsdp", scatter_dimension=dim, tiled=True)

    down_sum = scatter(contract(hidden_all, cotangent_all, 0, 0), 1).astype(jnp.float32)
    gate_sum = scatter(contract(hidden_in_all, gate_back_all, 0, 0), 0).astype(jnp.float32)
    up_sum = scatter(contract(hidden_in_all, up_back_all, 0, 0), 0).astype(jnp.float32)

    mid_part, hidden_gain_part = jax.vjp(rms_scale, mid, hidden_gain)[1](hidden_in_back)
    mid_back = cotangent.astype(jnp.float32) + mid_part
    mixer_rows = team_rows(mid_back.astype(low))

    lookup = partial(head_lookup, cosine_table=cosine_table, sine_table=sine_table)
    in_back = None
    query_gain_part = key_gain_part = 0.0
    mix_sums, output_sums = [], []
    for full, kept in zip(set_full, saved):
        query_raw, key_raw, query_rows, keys, value_rows, attended, log_total = kept
        attended_flat = attended.reshape(seq_length, query_width)
        output_sums.append(scatter(contract(mixer_rows, attended_flat, 0, 0), 0))
        attended_gradient = (
            jnp.dot(mixer_rows, full[:, mix_width:], preferred_element_type=jnp.float32)
            .astype(low)
            .reshape(seq_length, local_keys, each_group, head_size)
        )
        query_back, key_back, value_gradient = attend_backward(
            query_rows, keys, value_rows, allowed, log_total, attended, attended_gradient
        )
        query_back = query_back.reshape(seq_length, local_queries, head_size)
        query_raw_back, query_gain_add = jax.vjp(lookup, query_raw, query_norm_gain)[1](query_back)
        key_raw_back, key_gain_add = jax.vjp(lookup, key_raw, key_gain)[1](key_back)
        query_gain_part = query_gain_part + query_gain_add
        key_gain_part = key_gain_part + key_gain_add
        mix_low = jnp.concatenate(
            [
                query_raw_back.astype(low).reshape(seq_length, query_width),
                key_raw_back.astype(low).reshape(seq_length, key_width),
                value_gradient.reshape(seq_length, key_width),
            ],
            axis=1,
        )
        term = contract(mix_low, full[:, :mix_width], 1, 1)
        in_back = term if in_back is None else in_back + term
        mix_sums.append(scatter(contract(attention_rows, mix_low, 0, 0), 0))

    attention_in_back = team_sum(in_back)
    input_part, attention_gain_part = jax.vjp(rms_scale, input_float, attention_gain)[1](
        attention_in_back
    )
    input_gradient = (mid_back + input_part).astype(low)

    def home(parts):
        total = parts[0].astype(jnp.float32)
        for m in range(1, sets):
            moved = lax.ppermute(
                parts[m],
                "tp",
                [(i, (i // team + sets - m) % sets * team + i % team) for i in range(tp)],
            )
            total = total + moved.astype(jnp.float32)
        return total

    output_sum = home(output_sums).T
    mix_sum = home(mix_sums)
    query_sum = mix_sum[:, :query_width]
    key_sum = mix_sum[:, query_width : query_width + key_width]
    value_sum = mix_sum[:, query_width + key_width :]

    gains = jnp.concatenate(
        [attention_gain_part, hidden_gain_part, query_gain_part, key_gain_part]
    )
    for axis, size in (("fsdp", fsdp), ("tp", tp)):
        bit = 1
        while bit < size:
            gains = gains + lax.ppermute(gains, axis, [(i, i ^ bit) for i in range(size)])
            bit *= 2
    return (
        layer_output,
        input_gradient,
        gains[:width],
        query_sum,
        key_sum,
        value_sum,
        gains[2 * width : 2 * width + head_size],
        gains[2 * width + head_size :],
        output_sum,
        gains[width : 2 * width],
        gate_sum,
        up_sum,
        down_sum,
    )


def solution(mesh):
    rows = P(("fsdp", "tp"), None)
    in_specs = (
        rows,
        P("fsdp", None),
        rows,
        P(),
        P("fsdp", "tp"),
        P("fsdp", "tp"),
        P("fsdp", "tp"),
        P(),
        P(),
        P("tp", "fsdp"),
        P(),
        P("fsdp", "tp"),
        P("fsdp", "tp"),
        P("tp", "fsdp"),
    )
    out_specs = (
        rows,
        rows,
        P(),
        P("fsdp", "tp"),
        P("fsdp", "tp"),
        P("fsdp", "tp"),
        P(),
        P(),
        P("tp", "fsdp"),
        P(),
        P("fsdp", "tp"),
        P("fsdp", "tp"),
        P("tp", "fsdp"),
    )
    sizes = (mesh.shape["fsdp"], mesh.shape["tp"])
    return jax.shard_map(
        partial(shards, sizes),
        mesh=mesh,
        in_specs=in_specs,
        out_specs=out_specs,
        check_vma=False,
    )
```

```python
import functools
import math

import jax
import jax.numpy as jnp
from jax import lax
from jax.experimental import pallas as pl
from jax.experimental.pallas import tpu as pltpu
from jax.sharding import PartitionSpec as P

EPSILON = 1e-06
THETA = 1000000.0
MASKED = -1e30


def rms_scale(value_rows, norm_gain):
    return (
        value_rows
        * lax.rsqrt(jnp.mean(value_rows * value_rows, axis=-1, keepdims=True) + EPSILON)
        * norm_gain
    )


def doc_starts(segments):
    length = segments.shape[-1]
    indices = jnp.arange(length, dtype=jnp.int32)
    leading = jnp.ones(segments.shape[:-1] + (1,), dtype=jnp.bool_)
    change = jnp.concatenate([leading, segments[..., 1:] != segments[..., :-1]], axis=-1)
    return lax.cummax(jnp.where(change, indices, jnp.int32(0)), axis=segments.ndim - 1)


def contract(left_side, right_side, left_dim, right_dim):
    return lax.dot_general(
        left_side,
        right_side,
        (((left_dim,), (right_dim,)), ((), ())),
        preferred_element_type=jnp.float32,
    )


def inverse_rms(rows):
    return lax.rsqrt(jnp.mean(rows * rows, axis=-1, keepdims=True) + EPSILON)


def head_columns(head, size):
    return slice(head * size, (head + 1) * size)


def mix_specs(full, rows, group, heads, size):
    width = full.shape[0]
    return [
        pl.BlockSpec((width, (group + 2) * size), lambda h: (0, h)),
        pl.BlockSpec((width, group * size), lambda h: (0, heads * (group + 2) // group + h)),
    ]


def table_specs(rows, size):
    return [
        pl.BlockSpec((rows, size), lambda h: (0, 0)),
        pl.BlockSpec((rows, size), lambda h: (0, 0)),
        pl.BlockSpec((1, size), lambda h: (0, 0)),
        pl.BlockSpec((1, size), lambda h: (0, 0)),
        pl.BlockSpec((rows, 1), lambda h: (0, 0)),
        pl.BlockSpec((rows, 1), lambda h: (0, 0)),
        pl.BlockSpec((1, rows), lambda h: (0, 0)),
    ]


def weights_of(query, key, allowed, size):
    scores = contract(query, key, 1, 1) * (1.0 / math.sqrt(size))
    exponent = jnp.exp(jnp.where(allowed, scores, MASKED))
    return exponent * (1.0 / jnp.sum(exponent, axis=-1, keepdims=True))


def once(shape):
    return pl.BlockSpec(shape, lambda h: (0, 0), pipeline_mode=pl.Buffered(1))


def sum_shapes(rows, width, own_rows, last):
    if not last:
        return [jax.ShapeDtypeStruct((rows, width), jnp.float32)]
    return [
        jax.ShapeDtypeStruct((own_rows, width), jnp.float32),
        jax.ShapeDtypeStruct((rows - own_rows, width), jnp.bfloat16),
    ]


def put_sum(head, heads, term, before_refs, total_ref, out_refs):
    @pl.when(head == 0)
    def _():
        total_ref[...] = term + before_refs[0][...] if before_refs else term

    @pl.when(head > 0)
    def _():
        total_ref[...] += term

    if len(out_refs) == 2:

        @pl.when(head == heads - 1)
        def _():
            own_rows = out_refs[0].shape[0]
            out_refs[0][...] = total_ref[:own_rows]
            out_refs[1][...] = total_ref[own_rows:].astype(jnp.bfloat16)


def mixer_forward(rows_in, full, tables, group, heads, before, own_rows, last):
    rows, width = rows_in.shape
    size = tables[0].shape[1]
    low = jnp.bfloat16
    wide, thin, kept = (group + 2) * size, group * size, (group + 1) * size

    def kernel(x_ref, w_ref, o_ref, cos_ref, sin_ref, qg_ref, kg_ref, tok_ref, lo_ref, col_ref,
               *refs):
        before_refs, refs = refs[: len(before)], refs[len(before) :]
        raw_ref, rot_ref, att_ref = refs[:3]
        sum_refs, total_ref = (refs[3:5], refs[5]) if last else (refs[3:4], refs[3])
        head = pl.program_id(0)
        raw = jnp.dot(x_ref[...], w_ref[...], preferred_element_type=jnp.float32)
        raw_ref[...] = raw[:, :kept]
        value = raw[:, kept:].astype(low)
        cosine, sine = cos_ref[...], sin_ref[...]
        turned = []
        for part in range(group + 1):
            vector = raw[:, head_columns(part, size)]
            gain = qg_ref[...] if part < group else kg_ref[...]
            vector = vector * inverse_rms(vector) * gain
            turned.append(
                (vector * cosine + pltpu.roll(vector, size // 2, 1) * sine).astype(low)
            )
        for part in range(group + 1):
            rot_ref[:, head_columns(part, size)] = turned[part]
        rot_ref[:, head_columns(group + 1, size)] = value
        allowed = (tok_ref[...] >= col_ref[...]) & (lo_ref[...] <= col_ref[...])
        for part in range(group):
            share = weights_of(turned[part], turned[group], allowed, size).astype(low)
            att_ref[:, head_columns(part, size)] = jnp.dot(
                share, value, preferred_element_type=jnp.float32
            ).astype(low)
        term = contract(att_ref[...], o_ref[...], 1, 1)
        put_sum(head, heads, term, before_refs, total_ref, sum_refs)

    sums = sum_shapes(rows, width, own_rows, last)

    return pl.pallas_call(
        kernel,
        out_shape=(
            jax.ShapeDtypeStruct((rows, heads * kept), jnp.float32),
            jax.ShapeDtypeStruct((rows, heads * wide), low),
            jax.ShapeDtypeStruct((rows, heads * thin), low),
            *sums,
        ),
        grid=(heads,),
        in_specs=[once((rows, width))]
        + mix_specs(full, rows, group, heads, size)
        + table_specs(rows, size)
        + [once((rows, width)) for _ in before],
        out_specs=(
            pl.BlockSpec((rows, kept), lambda h: (0, h)),
            pl.BlockSpec((rows, wide), lambda h: (0, h)),
            pl.BlockSpec((rows, thin), lambda h: (0, h)),
            *[once(item.shape) for item in sums],
        ),
        scratch_shapes=[pltpu.VMEM((rows, width), jnp.float32)] if last else [],
        cost_estimate=pl.CostEstimate(
            flops=2 * rows * heads * (width * (wide + thin) + 2 * rows * thin),
            bytes_accessed=2 * width * heads * (wide + thin) + 8 * rows * width,
            transcendentals=rows * rows * heads * group,
        ),
        name="mixer_forward",
    )(rows_in, full, full, *tables, *before)


def mixer_backward(
    back_rows, full, tables, raw, rotated, attended, group, heads, before, source, own_rows
):
    last = bool(source)
    rows, width = back_rows.shape
    size = tables[0].shape[1]
    low = jnp.bfloat16
    wide, thin, kept = (group + 2) * size, group * size, (group + 1) * size
    scale = 1.0 / math.sqrt(size)

    def kernel(g_ref, w_ref, o_ref, cos_ref, sin_ref, qg_ref, kg_ref, tok_ref, lo_ref, col_ref,
               raw_ref, rot_ref, att_ref, *refs):
        before_refs, refs = refs[: len(before)], refs[len(before) :]
        source_refs, refs = refs[: len(source)], refs[len(source) :]
        low_ref, gain_ref = refs[:2]
        sum_refs, total_ref = (refs[2:4], refs[5]) if last else (refs[2:3], refs[2])
        head = pl.program_id(0)

        @pl.when(head == 0)
        def _():
            gain_ref[...] = jnp.zeros_like(gain_ref)

        attended_back = jnp.dot(
            g_ref[...], o_ref[...], preferred_element_type=jnp.float32
        ).astype(low)
        key = rot_ref[:, head_columns(group, size)]
        value = rot_ref[:, head_columns(group + 1, size)]
        cosine, sine = cos_ref[...], sin_ref[...]
        allowed = (tok_ref[...] >= col_ref[...]) & (lo_ref[...] <= col_ref[...])

        def unturn(part, turned_back, gain, row):
            vector = raw_ref[:, head_columns(part, size)]
            back = turned_back * cosine + pltpu.roll(turned_back * sine, size // 2, 1)
            inverse = inverse_rms(vector)
            gain_ref[row : row + 1, :] += jnp.sum(
                back * vector * inverse, axis=0, keepdims=True
            )
            back = back * gain
            shift = jnp.mean(back * vector, axis=-1, keepdims=True) * inverse * inverse
            low_ref[:, head_columns(part, size)] = ((back - vector * shift) * inverse).astype(low)

        key_back = jnp.zeros((rows, size), jnp.float32)
        value_back = jnp.zeros((rows, size), jnp.float32)
        for part in range(group):
            query = rot_ref[:, head_columns(part, size)]
            back = attended_back[:, head_columns(part, size)]
            delta = jnp.sum(
                back.astype(jnp.float32)
                * att_ref[:, head_columns(part, size)].astype(jnp.float32),
                axis=-1,
                keepdims=True,
            )
            share = weights_of(query, key, allowed, size)
            score_back = (share * (contract(back, value, 1, 1) - delta)).astype(low)
            value_back += contract(share.astype(low), back, 0, 0)
            key_back += contract(score_back, query, 0, 0)
            query_back = jnp.dot(score_back, key, preferred_element_type=jnp.float32) * scale
            unturn(part, query_back, qg_ref[...], 0)
        unturn(group, key_back * scale, kg_ref[...], 1)
        low_ref[:, head_columns(group + 1, size)] = value_back.astype(low)
        term = contract(low_ref[...], w_ref[...], 1, 1)
        put_sum(head, heads, term, before_refs, total_ref, sum_refs)
        if last:

            @pl.when(head == heads - 1)
            def _():
                rows_float = source_refs[0][...].astype(jnp.float32)
                unit = rows_float * inverse_rms(rows_float)
                refs[4][...] = jnp.sum(total_ref[...] * unit, axis=0, keepdims=True)

    sums = sum_shapes(rows, width, own_rows, last)
    if last:
        sums.append(jax.ShapeDtypeStruct((1, width), jnp.float32))

    return pl.pallas_call(
        kernel,
        out_shape=(
            jax.ShapeDtypeStruct((rows, heads * wide), low),
            jax.ShapeDtypeStruct((8, size), jnp.float32),
            *sums,
        ),
        grid=(heads,),
        in_specs=[once((rows, width))]
        + mix_specs(full, rows, group, heads, size)
        + table_specs(rows, size)
        + [
            pl.BlockSpec((rows, kept), lambda h: (0, h)),
            pl.BlockSpec((rows, wide), lambda h: (0, h)),
            pl.BlockSpec((rows, thin), lambda h: (0, h)),
        ]
        + [once((rows, width)) for _ in before + source],
        out_specs=(
            pl.BlockSpec((rows, wide), lambda h: (0, h)),
            pl.BlockSpec((8, size), lambda h: (0, 0)),
            *[once(item.shape) for item in sums],
        ),
        scratch_shapes=[pltpu.VMEM((rows, width), jnp.float32)] if last else [],
        cost_estimate=pl.CostEstimate(
            flops=2 * rows * heads * (width * (wide + thin) + 5 * rows * thin),
            bytes_accessed=2 * width * heads * (wide + thin) + 8 * rows * width,
            transcendentals=rows * rows * heads * group,
        ),
        name="mixer_backward",
    )(back_rows, full, full, *tables, raw, rotated, attended, *before, *source)


def block_product(block_ids, block, lefts, rights, received, split):
    low = jnp.bfloat16
    count = block_ids.shape[0]
    out_width = sum(group[0].shape[1] for group in rights)
    flat = [piece for group in rights for piece in group]
    tokens = sum(piece.shape[0] for piece in lefts)
    rest = count - split

    def kernel(ids_ref, *refs):
        left_refs, refs = refs[: len(lefts)], refs[len(lefts) :]
        right_refs, refs = refs[: len(flat)], refs[len(flat) :]
        columns, taken = [], 0
        for group in rights:
            pieces = [ref[...] for ref in right_refs[taken : taken + len(group)]]
            columns.append(jnp.concatenate(pieces, axis=0) if len(pieces) > 1 else pieces[0])
            taken += len(group)
        left = [ref[...] for ref in left_refs]
        left = jnp.concatenate(left, axis=0) if len(left) > 1 else left[0]
        outs = refs[1:] if received is not None else refs
        at = 0
        for column in columns:
            span = slice(at, at + column.shape[1])
            at = span.stop
            total = contract(left, column, 0, 0)
            if received is not None:
                total = total + refs[0][:, span].astype(jnp.float32)
            if rest == 0:
                outs[0][:, span] = total.astype(low)
                continue

            @pl.when(pl.program_id(0) < split)
            def _(total=total, span=span):
                outs[0][:, span] = total.astype(low)

            @pl.when(pl.program_id(0) >= split)
            def _(total=total, span=span):
                outs[1][:, span] = total

    out_shape = [jax.ShapeDtypeStruct((split * block, out_width), low)]
    out_specs = [
        pl.BlockSpec((block, out_width), lambda i, ids: (jnp.minimum(i, split - 1), 0))
    ]
    if rest:
        out_shape.append(jax.ShapeDtypeStruct((rest * block, out_width), jnp.float32))
        out_specs.append(
            pl.BlockSpec((block, out_width), lambda i, ids: (jnp.maximum(i - split, 0), 0))
        )
    extra = [] if received is None else [received]
    return pl.pallas_call(
        kernel,
        out_shape=out_shape,
        grid_spec=pltpu.PrefetchScalarGridSpec(
            num_scalar_prefetch=1,
            grid=(count,),
            in_specs=[
                pl.BlockSpec((piece.shape[0], block), lambda i, ids: (0, ids[i]))
                for piece in lefts
            ]
            + [pl.BlockSpec(piece.shape, lambda i, ids: (0, 0)) for piece in flat]
            + [pl.BlockSpec((block, out_width), lambda i, ids: (i, 0)) for _ in extra],
            out_specs=out_specs,
        ),
        cost_estimate=pl.CostEstimate(
            flops=2 * tokens * count * block * out_width,
            bytes_accessed=2 * tokens * (count * block + out_width)
            + 4 * count * block * out_width,
            transcendentals=0,
        ),
        name="block_product",
    )(block_ids, *lefts, *flat, *extra)


def after(value, *others):
    return lax.optimization_barrier((value,) + others)[0]


class Chain:
    def __init__(self):
        self.last = None

    def gate(self, value):
        return value if self.last is None else after(value, self.last)

    def mark(self, value):
        self.last = value
        return value


def halving_masks(bits):
    if not bits:
        return [0]
    rest = halving_masks(bits[1:])
    return [bits[0] ^ mask for mask in rest] + rest


def block_orders(fsdp):
    bits = [1 << k for k in range(1, fsdp.bit_length() - 1)]
    orders = (bits, bits[::-1])
    chip = lax.axis_index("fsdp")
    even, odd = (jnp.array(halving_masks(b), jnp.int32) for b in orders)
    own = chip % 2 == 0
    return orders, chip ^ 1 ^ jnp.where(own, odd, even), chip ^ jnp.where(own, even, odd)


class Doubling:
    def __init__(self, fsdp, piece):
        self.size, self.piece = fsdp, piece
        self.orders, self.far_ids, self.near_ids = block_orders(fsdp)
        self.left = len(self.orders[0])
        self.start()

    def start(self):
        self.left -= 1
        if self.left >= 0:
            pairs = [(r, r ^ self.orders[r % 2][self.left]) for r in range(self.size)]
        else:
            pairs = [(r, r ^ 1) for r in range(self.size)]
        self.moved = lax.ppermute(self.piece, "fsdp", pairs)

    def next(self, token):
        self.piece = jnp.concatenate([after(self.moved, token), self.piece], axis=0)
        self.start()

    def whole(self, token):
        half, columns = self.piece.shape
        count = self.size // 2
        block = half // count

        def kernel(ids_ref, far_ref, near_ref, out_ref):
            @pl.when(pl.program_id(0) < count)
            def _():
                out_ref[...] = far_ref[...]

            @pl.when(pl.program_id(0) >= count)
            def _():
                out_ref[...] = near_ref[...]

        return pl.pallas_call(
            kernel,
            out_shape=jax.ShapeDtypeStruct((2 * half, columns), self.piece.dtype),
            grid_spec=pltpu.PrefetchScalarGridSpec(
                num_scalar_prefetch=1,
                grid=(2 * count,),
                in_specs=[
                    pl.BlockSpec((block, columns), lambda i, ids: (jnp.minimum(i, count - 1), 0)),
                    pl.BlockSpec((block, columns), lambda i, ids: (jnp.maximum(i - count, 0), 0)),
                ],
                out_specs=pl.BlockSpec((block, columns), lambda i, ids: (ids[i], 0)),
            ),
            cost_estimate=pl.CostEstimate(
                flops=0, bytes_accessed=8 * half * columns, transcendentals=0
            ),
            name="placed",
        )(jnp.concatenate([self.far_ids, self.near_ids]), after(self.moved, token), self.piece)


class Halving:
    def __init__(self, chain, fsdp, lefts, rights):
        self.chain, self.size = chain, fsdp
        self.lefts, self.rights = lefts, rights
        self.block = lefts[0].shape[1] // fsdp
        self.orders, self.sent_ids, self.kept_ids = block_orders(fsdp)
        self.step = 0

    def send(self):
        lefts = [self.chain.gate(self.lefts[0])] + self.lefts[1:]
        (sent,) = block_product(
            self.sent_ids, self.block, lefts, self.rights, None, self.size // 2
        )
        self.chain.mark(sent)
        self.moved = lax.ppermute(sent, "fsdp", [(r, r ^ 1) for r in range(self.size)])

    def keep(self):
        moved = self.chain.gate(self.moved)
        sent, self.rest = block_product(
            self.kept_ids, self.block, self.lefts, self.rights, moved, self.size // 4
        )
        self.chain.mark(sent)
        self.exchange(sent)

    def exchange(self, sent):
        self.moved = lax.ppermute(
            sent,
            "fsdp",
            [(r, r ^ self.orders[r % 2][self.step]) for r in range(self.size)],
        )
        self.step += 1

    def add(self):
        total = self.rest + self.chain.gate(self.moved).astype(jnp.float32)
        if self.step == len(self.orders[0]):
            self.chain.mark(total)
            return total
        half = total.shape[0] // 2
        sent, self.rest = total[:half].astype(jnp.bfloat16), total[half:]
        self.chain.mark(sent)
        self.exchange(sent)
        return None

    def finish(self):
        total = None
        while total is None:
            total = self.add()
        return total


def shards(
    sizes,
    layer_input,
    segments,
    cotangent,
    attention_gain,
    query_weight,
    key_matrix,
    value_matrix,
    query_norm_gain,
    key_gain,
    output_matrix,
    hidden_gain,
    gate_weight,
    up_weight,
    down_weight,
):
    fsdp, tp = sizes
    low = jnp.bfloat16
    own_rows, width = layer_input.shape
    seq_count, seq_length = segments.shape
    size = query_norm_gain.shape[0]
    team = tp // seq_count
    sets = seq_count
    me = lax.axis_index("tp")
    place = me % team
    chain = Chain()

    def hop(value):
        return lax.ppermute(value, "tp", [(i, (i + 1) % tp) for i in range(tp)])

    def team_hop(value, step):
        return lax.ppermute(
            value, "tp", [(i, i // team * team + (i + step) % team) for i in range(tp)]
        )

    def team_rows(own):
        return jnp.concatenate([own] + [team_hop(own, step) for step in range(1, team)], axis=0)

    def team_send(others):
        return [
            team_hop(others[k * own_rows : (k + 1) * own_rows], team - 1 - k)
            for k in range(team - 1)
        ]

    def total_of(own, moved):
        for part in moved:
            own = own + part.astype(jnp.float32)
        return own

    def ring_rows(own, tokens):
        blocks = [own]
        for _, token in zip(range(1, tp), tokens):
            blocks.append(hop(blocks[-1] if token is None else after(blocks[-1], token)))
        return blocks

    query_width = query_weight.shape[1]
    key_width = key_matrix.shape[1]
    mix_width = query_width + 2 * key_width
    heads = key_width // size
    group = query_width // key_width
    thin = group * size

    source = team_rows(layer_input)
    columns = []
    for head in range(heads):
        columns += [
            query_weight[:, head_columns(head, thin)],
            key_matrix[:, head_columns(head, size)],
            value_matrix[:, head_columns(head, size)],
        ]
    own_set = jnp.concatenate(columns + [output_matrix.T], axis=1)
    weight_sets = [own_set] + [
        lax.ppermute(
            own_set,
            "tp",
            [(i, (i // team + m) % sets * team + i % team) for i in range(tp)],
        )
        for m in range(1, sets)
    ]
    weight_sets[1:] = [after(w, source) for w in weight_sets[1:]]
    set_full = [lax.all_gather(w, "fsdp", axis=0, tiled=True) for w in weight_sets]
    down_full = lax.all_gather(after(down_weight, *weight_sets), "fsdp", axis=1, tiled=True)
    gate_gather = Doubling(fsdp, gate_weight)
    up_gather = Doubling(fsdp, up_weight)

    source_float = source.astype(jnp.float32)
    input_float = layer_input.astype(jnp.float32)
    attention_rows = rms_scale(source_float, attention_gain).astype(low)

    own_starts = doc_starts(lax.dynamic_index_in_dim(segments, me // team, 0, keepdims=False))
    firsts = [(place + team - step) % team * own_rows for step in range(team)]
    tokens = jnp.concatenate([first + jnp.arange(own_rows, dtype=jnp.int32) for first in firsts])
    starts = jnp.concatenate(
        [lax.dynamic_slice_in_dim(own_starts, first, own_rows) for first in firsts]
    )
    exponents = jnp.arange(size // 2, dtype=jnp.float32) * (-2.0 / size)
    frequencies = jnp.power(jnp.float32(THETA), exponents)
    angles = (tokens - starts).astype(jnp.float32)[:, None] * frequencies
    cosine, sine = jnp.cos(angles), jnp.sin(angles)
    tables = (
        jnp.concatenate([cosine, cosine], axis=1),
        jnp.concatenate([-sine, sine], axis=1),
        query_norm_gain[None],
        key_gain[None],
        tokens[:, None],
        starts[:, None],
        tokens[None],
    )

    for gather in (gate_gather, up_gather):
        gather.next(attention_rows)
    saved, mixed = [], []
    for m, full in enumerate(set_full):
        raw, rotated, attended, *mixed = mixer_forward(
            chain.gate(attention_rows), full, tables, group, heads, mixed, own_rows, m == sets - 1
        )
        chain.mark(attended)
        saved.append((raw, rotated, attended))
        if m == 0:
            for gather in (gate_gather, up_gather):
                while gather.left >= 0:
                    gather.next(attended)
    moved_mixed = team_send(mixed[1])
    gate_full, up_full = (gather.whole(mixed[1]) for gather in (gate_gather, up_gather))
    mid = input_float + total_of(mixed[0], moved_mixed)
    hidden_in = rms_scale(mid, hidden_gain).astype(low)

    cotangent_blocks = ring_rows(
        cotangent, [weight_sets[-1], saved[0][2]] + [saved[-1][2]] * (tp - 3)
    )
    hidden_blocks = ring_rows(after(hidden_in, cotangent_blocks[-1]), [None] * tp)
    in_parts, hiddens, gate_backs, up_backs = [], [], [], []
    for cotangent_rows, hidden_rows in zip(cotangent_blocks, hidden_blocks):
        hidden_rows = chain.gate(hidden_rows)
        gate_value = jnp.dot(hidden_rows, gate_full, preferred_element_type=jnp.float32)
        up_value = jnp.dot(hidden_rows, up_full, preferred_element_type=jnp.float32)
        hidden_back = contract(cotangent_rows, down_full, 1, 1)
        sigmoid = jax.nn.sigmoid(gate_value)
        hidden = (gate_value * sigmoid * up_value).astype(low)
        gate_back = (
            hidden_back * up_value * sigmoid * (1.0 + gate_value * (1.0 - sigmoid))
        ).astype(low)
        up_back = (hidden_back * gate_value * sigmoid).astype(low)
        hiddens.append(hidden)
        gate_backs.append(gate_back)
        up_backs.append(up_back)
        in_parts.append(
            chain.mark(contract(gate_back, gate_full, 1, 1) + contract(up_back, up_full, 1, 1))
        )

    down_grad = Halving(chain, fsdp, cotangent_blocks, [hiddens])
    gate_grad = Halving(chain, fsdp, hidden_blocks, [gate_backs])
    up_grad = Halving(chain, fsdp, hidden_blocks, [up_backs])
    fillers = [down_grad.send, gate_grad.send, down_grad.keep, up_grad.send]
    carried = in_parts[1]
    for step in range(2, tp + 1):
        arrived = hop(carried.astype(low))
        if step > 2:
            for fill in fillers[:2]:
                fill()
            fillers = fillers[2:]
        carried = chain.mark(chain.gate(arrived).astype(jnp.float32) + in_parts[step % tp])
    hidden_in_back = carried

    mid_part, hidden_gain_part = jax.vjp(rms_scale, mid, hidden_gain)[1](hidden_in_back)
    mid_back = cotangent.astype(jnp.float32) + mid_part
    mixer_own = chain.mark(mid_back.astype(low))
    mixer_rows = team_rows(mixer_own)
    for fill in fillers + [gate_grad.keep, up_grad.keep]:
        fill()

    out_parts = [
        jnp.dot(hidden, down_full, preferred_element_type=jnp.float32) for hidden in hiddens
    ]
    out_moved = [hop(after(out_parts[1].astype(low), mixer_rows))]

    def out_step():
        step = len(out_moved) + 1
        total = chain.gate(out_moved[-1]).astype(jnp.float32) + out_parts[step % tp]
        if step < tp:
            out_moved.append(hop(chain.mark(total.astype(low))))
        return total

    in_back, gain_parts = [], None
    mix_grads = [None] * sets
    for m in list(range(1, sets)) + [0]:
        raw, rotated, attended = saved[m]
        mix_low, gain_add, *in_back = mixer_backward(
            chain.gate(mixer_rows),
            set_full[m],
            tables,
            raw,
            rotated,
            attended,
            group,
            heads,
            in_back,
            [source] if m == 0 else [],
            own_rows,
        )
        chain.mark(mix_low)
        gain_parts = gain_add if gain_parts is None else gain_parts + gain_add
        mix_grads[m] = Halving(chain, fsdp, [attention_rows], [[mix_low]])
        if m > 0:
            mix_grads[m].send()
        if m == 1:
            down_grad.add()
            out_step()
    own_back, others_back, attention_gain_part = in_back
    moved_back = team_send(others_back)
    output_grad = Halving(chain, fsdp, [mixer_rows], [[kept[2]] for kept in saved])
    mix_grads[0].send()
    for m in range(1, sets):
        mix_grads[m].keep()
    output_grad.send()
    gate_grad.add()
    up_grad.add()
    mix_grads[0].keep()
    output_grad.keep()
    down_sum = down_grad.finish()
    while len(out_moved) < tp - 1:
        out_step()

    gains = jnp.concatenate(
        [attention_gain_part[0], hidden_gain_part, gain_parts[0], gain_parts[1]]
    )
    for axis, extent in (("fsdp", fsdp), ("tp", tp)):
        bit = 1
        while bit < extent:
            moved = lax.ppermute(gains, axis, [(i, i ^ bit) for i in range(extent)])
            gains = chain.mark(gains + chain.gate(moved))
            bit *= 2

    attention_in_back = total_of(own_back, [chain.gate(part) for part in moved_back])
    input_part = jax.vjp(lambda rows: rms_scale(rows, attention_gain), input_float)[1](
        attention_in_back
    )[0]
    input_gradient = chain.mark((mid_back + input_part).astype(low))

    for grad in mix_grads[1:] + [output_grad, mix_grads[0]]:
        if grad.step < len(grad.orders[0]):
            grad.add()
    gate_sum, up_sum = (grad.finish() for grad in (gate_grad, up_grad))
    mix_sums = [mix_grads[m].finish() for m in range(1, sets)]
    output_parts = output_grad.finish()
    mix_sums = [mix_grads[0].finish()] + mix_sums
    output_parts = [output_parts[:, head_columns(m, query_width)] for m in range(sets)]
    layer_output = (mid + out_step()).astype(low)

    total = jnp.concatenate([mix_sums[0], output_parts[0]], axis=1)
    for m in range(1, sets):
        moved = lax.ppermute(
            jnp.concatenate([mix_sums[m], output_parts[m]], axis=1).astype(low),
            "tp",
            [(i, (i // team + sets - m) % sets * team + i % team) for i in range(tp)],
        )
        total = total + moved.astype(jnp.float32)
    wide = thin + 2 * size
    query_sum, key_sum, value_sum = (
        jnp.concatenate(
            [total[:, head * wide + at : head * wide + at + span] for head in range(heads)],
            axis=1,
        )
        for at, span in ((0, thin), (thin, size), (thin + size, size))
    )
    output_sum = total[:, mix_width:].T

    return (
        layer_output,
        input_gradient,
        gains[:width],
        query_sum,
        key_sum,
        value_sum,
        gains[2 * width : 2 * width + size],
        gains[2 * width + size :],
        output_sum,
        gains[width : 2 * width],
        gate_sum,
        up_sum,
        down_sum.T,
    )


def solution(mesh):
    rows = P(("fsdp", "tp"), None)
    by_row, by_column = P("fsdp", "tp"), P("tp", "fsdp")
    in_specs = (
        (rows, P("fsdp", None), rows, P())
        + (by_row,) * 3
        + (P(), P(), by_column, P(), by_row, by_row, by_column)
    )
    out_specs = (
        (rows, rows, P())
        + (by_row,) * 3
        + (P(), P(), by_column, P(), by_row, by_row, by_column)
    )
    return jax.shard_map(
        functools.partial(shards, (mesh.shape["fsdp"], mesh.shape["tp"])),
        mesh=mesh,
        in_specs=in_specs,
        out_specs=out_specs,
        check_vma=False,
    )
```
